512 devices in a mesh: tm: 16 (over z_lo, y), series: 32 (over z_hi, x, core).
Axes of the slice: x: 4, y: 4, z: 16 (z_hi: 4, z_lo: 4; z = z_hi * 4 + z_lo), core: 2. Of those that a mesh axis runs over, the one named last changes fastest.
Arguments:
- inputs: bfloat16 [64, 8192, 512], P('series', 'tm'), may hold values from -6 to 6
- cotangent: bfloat16 [64, 8192, 512], P('series', 'tm'), may hold values from -6 to 6
- taps: int32 [3], replicated, may hold values from 0 to 128, as said below
- weight: float32 [1536, 512], P('series'), may hold values from -0.15625 to 0.15625
- moment_one: float32 [1536, 512], P('series'), may hold values from -10 to 10
- second_moment_state: float32 [1536, 512], P('series'), may hold values from 1 to 100
Outputs:
- grad_input: bfloat16 [64, 8192, 512], P('series', 'tm')
- new_weight: float32 [1536, 512], P('series')
- new_moment_one: float32 [1536, 512], P('series')
- new_moment_two: float32 [1536, 512], P('series')
The draws below stay inside these ranges and needn't reach their ends.
Inputs may be any that keep to these rules, and one draw needn't show every extreme that they name: taps[0] is 0, taps[2] is 128, and taps[1] lies strictly between them.
All inputs are finite; a program needn't handle non-finite values.
Results may differ from the reference program's by a relative error of at most 0.0045.
Values may be sent and summed in bfloat16 or wider, within the bound.
No kernel may reach another device: no remote copies, remote signals or barrier semaphores. Data moves between devices by JAX's collectives and lax.ppermute only.
A program may use at most 64 MiB of HBM per device.

```python
import math
import jax
import jax.numpy as jnp
from jax import lax

C = 512
KERNEL_TAPS = 3
DILATION_GAP = 64
SERIES = 64
WINDOW = 8192


def draw_taps(key, part):
    center_part = jax.random.randint(key, (1,), 1, 2 * DILATION_GAP).astype(jnp.int32)
    return jnp.concatenate([jnp.zeros((1,), jnp.int32), center_part, jnp.full((1,), 2 * DILATION_GAP, jnp.int32)])


def level_of(rng, extent, split, smallest, top_value):
    factor_of = 1.0
    for dim, shards_of in split:
        draws = jax.random.uniform(jax.random.fold_in(jax.random.fold_in(rng, 6), dim), (shards_of,), jnp.float32, smallest / len(split), top_value / len(split))
        factor_of = factor_of * jnp.repeat(jnp.exp(draws), extent[dim] // shards_of).reshape((-1,) + (1,) * (len(extent) - 1 - dim))
    return factor_of


def scatter_about(rng, shape, deviation, bound, split=(), held_as=jnp.bfloat16):
    array = deviation * jax.random.normal(rng, shape, jnp.float32)
    if split:
        array = array * level_of(rng, shape, split, -0.22, 0.18)
    return jnp.clip(array, -bound, bound).astype(held_as)


def setup_inputs(seed: int = 0) -> dict:
    seeds = jax.random.split(jax.random.key(seed), 7)
    return {
        "inputs": scatter_about(seeds[0], (SERIES, WINDOW, C), 1.0, 6.0, ((0, 32), (1, 16))),
        "cotangent": scatter_about(seeds[1], (SERIES, WINDOW, C), 1.0, 6.0, ((0, 32), (1, 16))),
        "taps": draw_taps(jax.random.fold_in(seeds[6], 71), 0),
        "weight": scatter_about(seeds[3], (KERNEL_TAPS * C, C), (KERNEL_TAPS * C) ** -0.5, 0.15625, ((0, 32),), jnp.float32),
        "moment_one": scatter_about(seeds[4], (KERNEL_TAPS * C, C), 2.0, 10.0, ((0, 32),), jnp.float32),
        "second_moment_state": jnp.clip(jnp.exp(math.log(100.0) - 4.6051702 * jax.random.uniform(seeds[5], (KERNEL_TAPS * C, C), jnp.float32) ** level_of(seeds[5], (KERNEL_TAPS * C, C), ((0, 32),), -0.2, 0.2)), 1.0, 100.0),
    }


def adamw(weight, grad, moment_one, second_moment_state):
    first = 0.9 * moment_one + 0.1 * grad
    second = 0.999 * second_moment_state + 0.001 * grad * grad
    unbiased_one = first / (1.0 - 0.9 ** 10)
    unbiased_two = second / (1.0 - 0.999 ** 10)
    updated = weight - 0.01 * (unbiased_one / (jnp.sqrt(unbiased_two) + 1e-08) + 0.1 * weight)
    return (updated, first, second)

def reference(inputs, cotangent, taps, weight, moment_one, second_moment_state):
    receptive_span = (KERNEL_TAPS - 1) * DILATION_GAP
    wcast = weight.astype(jnp.bfloat16)

    def one_series(grad, pair):
        seq_in, seq_up = pair
        extended = jnp.concatenate([jnp.zeros((receptive_span, C), jnp.bfloat16), seq_in], 0)
        stacked = jnp.concatenate([lax.dynamic_slice_in_dim(extended, (receptive_span - taps[k]).astype(jnp.int32), WINDOW, 0) for k in range(KERNEL_TAPS)], 1)
        pre = jnp.dot(stacked, wcast, preferred_element_type=jnp.float32)
        sig = jax.nn.sigmoid(pre)
        dpre = (seq_up.astype(jnp.float32) * (sig * (1.0 + pre * (1.0 - sig)))).astype(jnp.bfloat16)
        later = jnp.concatenate([dpre, jnp.zeros((receptive_span, C), jnp.bfloat16)], 0)
        result = seq_up.astype(jnp.float32)
        for k in range(KERNEL_TAPS):
            moved = lax.dynamic_slice_in_dim(later, taps[k].astype(jnp.int32), WINDOW, 0)
            result = result + jnp.dot(moved, wcast[k * C:(k + 1) * C].T, preferred_element_type=jnp.float32)
        grad = grad + lax.dot_general(stacked, dpre, (((0,), (0,)), ((), ())), preferred_element_type=jnp.float32)
        return (grad, result.astype(jnp.bfloat16))
    grad, grad_input = lax.scan(one_series, jnp.zeros((KERNEL_TAPS * C, C), jnp.float32), (inputs, cotangent))
    new_weight, new_moment_one, new_moment_two = adamw(weight, grad, moment_one, second_moment_state)
    return (grad_input, new_weight, new_moment_one, new_moment_two)
```

```python
import jax
import jax.numpy as jnp
from jax import lax
from jax.sharding import Mesh
from jax.sharding import PartitionSpec as P

DILATION_GAP = 64
TM = ("z_lo", "y")
SERIES = ("z_hi", "x", "core")
PLANE = ("x", "y")
LINE = ("z_hi", "z_lo")
LANES = 128


def passed_along(array, by):
    size = lax.axis_size(TM)
    pairs = [(i, i + by) for i in range(size) if 0 <= i + by < size]
    return lax.ppermute(array, TM, pairs)


def gathered(piece, axes):
    size = lax.axis_size(axes)
    return lax.all_to_all(jnp.broadcast_to(piece[None], (size,) + piece.shape), axes, 0, 0)


def swapped(array):
    return lax.ppermute(array, "core", [(0, 1), (1, 0)])


def gather_weight(shard):
    rows, width = shard.shape
    z_hi, z_lo = lax.axis_size("z_hi"), lax.axis_size("z_lo")
    x, y = lax.axis_size("x"), lax.axis_size("y")
    part, lanes = rows // z_lo, width // y
    piece = lax.dynamic_slice(
        shard, (lax.axis_index("z_lo") * part, lax.axis_index("y") * lanes), (part, lanes)
    )
    line = gathered(piece, LINE).reshape(z_hi * rows, lanes)
    mine = gathered(line, PLANE)
    other = swapped(mine)
    first = lax.axis_index("core") == 0
    both = jnp.stack([jnp.where(first, mine, other), jnp.where(first, other, mine)])
    both = both.reshape(2, x, y, z_hi, rows, lanes).transpose(3, 1, 0, 4, 2, 5)
    return both.reshape(z_hi * x * 2 * rows, width)


def reduce_grad(grad):
    z_hi, z_lo = lax.axis_size("z_hi"), lax.axis_size("z_lo")
    x, y = lax.axis_size("x"), lax.axis_size("y")
    total, width = grad.shape
    rows, lanes = total // (z_hi * x * 2), width // y
    halves = grad.reshape(z_hi, x, 2, rows, width)
    core = lax.axis_index("core")
    keep = lax.dynamic_index_in_dim(halves, core, 2, keepdims=False)
    give = lax.dynamic_index_in_dim(halves, 1 - core, 2, keepdims=False)
    chip = keep + swapped(give)
    chunks = chip.reshape(z_hi, x, rows, y, lanes).transpose(1, 3, 0, 2, 4)
    chunks = chunks.reshape(x * y, z_hi * rows, lanes).astype(jnp.bfloat16)
    plane = jnp.sum(lax.all_to_all(chunks, PLANE, 0, 0).astype(jnp.float32), 0)
    line = plane.reshape(z_hi * z_lo, rows // z_lo, lanes)
    piece = jnp.sum(lax.all_to_all(line, LINE, 0, 0), 0)
    pieces = gathered(piece, TM).reshape(z_lo, y, rows // z_lo, lanes)
    return pieces.transpose(0, 2, 1, 3).reshape(rows, width)


def adamw(weight, grad, moment_one, second_moment_state):
    first = 0.9 * moment_one + 0.1 * grad
    second = 0.999 * second_moment_state + 0.001 * grad * grad
    unbiased_one = first / (1.0 - 0.9**10)
    unbiased_two = second / (1.0 - 0.999**10)
    updated = weight - 0.01 * (unbiased_one / (jnp.sqrt(unbiased_two) + 1e-08) + 0.1 * weight)
    return (updated, first, second)


def body(inputs, cotangent, taps, weight, moment_one, second_moment_state):
    series_n, time_n, width = inputs.shape
    tap_count = taps.shape[0]
    receptive_span = (tap_count - 1) * DILATION_GAP
    rows = series_n * time_n
    wide = gather_weight(weight.astype(jnp.bfloat16))
    earlier = passed_along(inputs[:, time_n - receptive_span :, :], 1)
    extended = jnp.concatenate([earlier, inputs], 1)
    shifted = [
        lax.dynamic_slice_in_dim(extended, receptive_span - taps[k], time_n, 1)
        for k in range(tap_count)
    ]
    stacked = jnp.concatenate(shifted, 2).reshape(rows, tap_count * width)
    pre = jnp.dot(stacked, wide, preferred_element_type=jnp.float32)
    sig = jax.nn.sigmoid(pre)
    upstream = cotangent.reshape(rows, width)
    dpre_flat = (upstream.astype(jnp.float32) * (sig * (1.0 + pre * (1.0 - sig)))).astype(
        jnp.bfloat16
    )
    dpre = dpre_flat.reshape(series_n, time_n, width)
    grad = lax.dot_general(
        stacked, dpre_flat, (((0,), (0,)), ((), ())), preferred_element_type=jnp.float32
    )
    grad_shard = reduce_grad(grad)
    ahead = passed_along(dpre[:, :receptive_span, :], -1)
    later = jnp.concatenate([dpre, ahead], 1)
    result = upstream.astype(jnp.float32)
    for k in range(tap_count):
        moved = lax.dynamic_slice_in_dim(later, taps[k], time_n, 1).reshape(rows, width)
        result = result + lax.dot_general(
            moved,
            wide[k * width : (k + 1) * width],
            (((1,), (1,)), ((), ())),
            preferred_element_type=jnp.float32,
        )
    grad_input = result.astype(jnp.bfloat16).reshape(series_n, time_n, width)
    new_weight, new_moment_one, new_moment_two = adamw(
        weight, grad_shard, moment_one, second_moment_state
    )
    return (grad_input, new_weight, new_moment_one, new_moment_two)


def solution(mesh):
    torus = Mesh(mesh.devices.reshape(4, 4, 4, 4, 2), TM + SERIES)
    tokens = P(SERIES, TM, None)
    rows = P(SERIES, None)
    return jax.shard_map(
        body,
        mesh=torus,
        in_specs=(tokens, tokens, P(), rows, rows, rows),
        out_specs=(tokens, rows, rows, rows),
        check_vma=False,
    )
```

```python
import jax
import jax.numpy as jnp
from jax import lax
from jax.experimental import pallas as pl
from jax.experimental.pallas import tpu as pltpu
from jax.sharding import Mesh
from jax.sharding import PartitionSpec as P

DILATION_GAP = 64
TM = ("z_lo", "y")
SERIES = ("z_hi", "x", "core")
PLANE = ("x", "y")
LINE = ("z_hi", "z_lo")
BLOCK_ROWS = 48


def passed_along(array, by):
    size = lax.axis_size(TM)
    pairs = [(i, i + by) for i in range(size) if 0 <= i + by < size]
    return lax.ppermute(array, TM, pairs)


def gathered(piece, axes):
    size = lax.axis_size(axes)
    return lax.all_to_all(jnp.broadcast_to(piece[None], (size,) + piece.shape), axes, 0, 0)


def swapped(array):
    return lax.ppermute(array, "core", [(0, 1), (1, 0)])


def gather_weight(shard):
    rows, width = shard.shape
    z_hi, z_lo = lax.axis_size("z_hi"), lax.axis_size("z_lo")
    part, lanes = rows // z_lo, width // lax.axis_size("y")
    piece = lax.dynamic_slice(
        shard, (lax.axis_index("z_lo") * part, lax.axis_index("y") * lanes), (part, lanes)
    )
    line = gathered(piece, LINE).reshape(z_hi * rows, lanes)
    mine = gathered(line, PLANE)
    return mine, swapped(mine)


def layer_kernel(
    core_ref, mine_ref, other_ref, near_ref, mid_ref, up_ref, dpre_ref, wide_ref, keep_ref, give_ref, acc_ref
):
    series_n, time_n, width = up_ref.shape
    span = near_ref.shape[1] - time_n
    own_n = time_n - span
    planes, line_rows, lanes = mine_ref.shape
    y = width // lanes
    x = planes // y
    rows = BLOCK_ROWS
    z_hi = line_rows // rows
    core = core_ref[0]

    def blocks():
        for h in range(z_hi):
            for i in range(x):
                for j in range(y):
                    yield h, (h * x + i) * 2 * rows, i * y + j, j * lanes

    own, far = core * rows, (1 - core) * rows
    for h, base, p, lane in blocks():
        here = pl.ds(pl.multiple_of(base + own, 16), rows)
        there = pl.ds(pl.multiple_of(base + far, 16), rows)
        wide_ref[here, lane : lane + lanes] = mine_ref[p, h * rows : (h + 1) * rows, :]
        wide_ref[there, lane : lane + lanes] = other_ref[p, h * rows : (h + 1) * rows, :]
    chunk = 128
    for s in range(series_n):
        for m in range(0, time_n, chunk):
            taken = (
                near_ref[s, span + m : span + m + chunk, :],
                mid_ref[s, m : m + chunk, :],
                near_ref[s, m : m + chunk, :],
            )
            pre = sum(
                jnp.dot(
                    t,
                    wide_ref[k * width : (k + 1) * width, :],
                    preferred_element_type=jnp.float32,
                )
                for k, t in enumerate(taken)
            )
            sig = jax.nn.sigmoid(pre)
            up = up_ref[s, m : m + chunk, :].astype(jnp.float32)
            dpre_ref[s, m : m + chunk, :] = (up * (sig * (1.0 + pre * (1.0 - sig)))).astype(
                jnp.bfloat16
            )
    for k in range(3):
        for s in range(series_n):
            taken = (
                near_ref[s, span : span + own_n, :],
                mid_ref[s, :own_n, :],
                near_ref[s, :own_n, :],
            )[k]
            part = lax.dot_general(
                taken,
                dpre_ref[s, :own_n, :],
                (((0,), (0,)), ((), ())),
                preferred_element_type=jnp.float32,
            )
            if s == 0:
                acc_ref[k * width : (k + 1) * width, :] = part
            else:
                acc_ref[k * width : (k + 1) * width, :] += part
    for h, base, p, lane in blocks():
        here = pl.ds(pl.multiple_of(base + own, 8), rows)
        there = pl.ds(pl.multiple_of(base + far, 8), rows)
        keep_ref[p, h * rows : (h + 1) * rows, :] = acc_ref[here, lane : lane + lanes]
        give_ref[p, h * rows : (h + 1) * rows, :] = acc_ref[there, lane : lane + lanes]


def layer(core, mine, other, near, mid, up):
    planes, line_rows, lanes = mine.shape
    width = up.shape[-1]
    total = 2 * planes * line_rows * lanes // width
    half = jax.ShapeDtypeStruct(mine.shape, jnp.float32)
    spec = pl.BlockSpec(memory_space=pltpu.VMEM)
    return pl.pallas_call(
        layer_kernel,
        in_specs=[pl.BlockSpec(memory_space=pltpu.SMEM)] + [spec] * 5,
        out_specs=[spec] * 4,
        out_shape=[
            jax.ShapeDtypeStruct(up.shape, jnp.bfloat16),
            jax.ShapeDtypeStruct((total, width), jnp.bfloat16),
            half,
            half,
        ],
        scratch_shapes=[pltpu.VMEM((total, width), jnp.float32)],
        compiler_params=pltpu.CompilerParams(vmem_limit_bytes=40 * 1024 * 1024),
        name="layer",
    )(core, mine, other, near, mid, up)


def reduce_grad(keep, give, rows):
    z_hi, z_lo, y = lax.axis_size("z_hi"), lax.axis_size("z_lo"), lax.axis_size("y")
    lanes = keep.shape[-1]
    chunks = (keep + swapped(give)).astype(jnp.bfloat16)
    plane = jnp.sum(lax.all_to_all(chunks, PLANE, 0, 0).astype(jnp.float32), 0)
    line = plane.reshape(z_hi * z_lo, rows // z_lo, lanes)
    piece = jnp.sum(lax.all_to_all(line, LINE, 0, 0), 0)
    pieces = gathered(piece, TM).reshape(z_lo, y, rows // z_lo, lanes)
    return pieces.transpose(0, 2, 1, 3).reshape(rows, y * lanes), plane


def adamw(weight, grad, moment_one, second_moment_state):
    first = 0.9 * moment_one + 0.1 * grad
    second = 0.999 * second_moment_state + 0.001 * grad * grad
    unbiased_one = first / (1.0 - 0.9**10)
    unbiased_two = second / (1.0 - 0.999**10)
    updated = weight - 0.01 * (unbiased_one / (jnp.sqrt(unbiased_two) + 1e-08) + 0.1 * weight)
    return (updated, first, second)


def body(inputs, cotangent, taps, weight, moment_one, second_moment_state):
    series_n, time_n, width = inputs.shape
    span = 2 * DILATION_GAP
    mine, other = gather_weight(weight.astype(jnp.bfloat16))
    earlier = passed_along(inputs[:, time_n - span :, :], 1)
    later = passed_along(jnp.stack([inputs[:, :span, :], cotangent[:, :span, :]]), -1)
    near = jnp.concatenate([earlier, inputs, later[0]], 1)
    up = jnp.concatenate([cotangent, later[1]], 1)
    mid = lax.dynamic_slice_in_dim(near, span - taps[1], time_n + span, 1)
    core = lax.axis_index("core").astype(jnp.int32).reshape(1)
    dpre, wide, keep, give = layer(core, mine, other, near, mid, up)
    grad_shard, plane = reduce_grad(keep, give, weight.shape[0])
    dpre, plane = lax.optimization_barrier((dpre, plane))
    result = cotangent.reshape(-1, width).astype(jnp.float32)
    for k, moved in enumerate(
        (dpre[:, :time_n], lax.dynamic_slice_in_dim(dpre, taps[1], time_n, 1), dpre[:, span:])
    ):
        result = result + lax.dot_general(
            moved.reshape(-1, width),
            wide[k * width : (k + 1) * width],
            (((1,), (1,)), ((), ())),
            preferred_element_type=jnp.float32,
        )
    grad_input = result.astype(jnp.bfloat16).reshape(series_n, time_n, width)
    new_weight, new_moment_one, new_moment_two = adamw(
        weight, grad_shard, moment_one, second_moment_state
    )
    return (grad_input, new_weight, new_moment_one, new_moment_two)


def solution(mesh):
    torus = Mesh(mesh.devices.reshape(4, 4, 4, 4, 2), TM + SERIES)
    tokens = P(SERIES, TM, None)
    rows = P(SERIES, None)
    return jax.shard_map(
        body,
        mesh=torus,
        in_specs=(tokens, tokens, P(), rows, rows, rows),
        out_specs=(tokens, rows, rows, rows),
        check_vma=False,
    )
```

```python
import jax
import jax.numpy as jnp
from jax import lax
from jax.experimental import pallas as pl
from jax.experimental.pallas import tpu as pltpu
from jax.sharding import Mesh
from jax.sharding import PartitionSpec as P

DILATION_GAP = 64
TM = ("z_lo", "y")
SERIES = ("z_hi", "x", "core")
PLANE = ("x", "y")
LINE = ("z_hi", "z_lo")
BLOCK_ROWS = 48


def passed_along(array, by):
    size = lax.axis_size(TM)
    pairs = [(i, i + by) for i in range(size) if 0 <= i + by < size]
    return lax.ppermute(array, TM, pairs)


def gathered(piece, axes):
    size = lax.axis_size(axes)
    return lax.all_to_all(jnp.broadcast_to(piece[None], (size,) + piece.shape), axes, 0, 0)


def swapped(array):
    return lax.ppermute(array, "core", [(0, 1), (1, 0)])


def away(array):
    return pltpu.with_memory_space_constraint(array, pltpu.HBM)


NEAR = pl.BlockSpec(memory_space=pltpu.VMEM)
AWAY = pl.BlockSpec(memory_space=pltpu.HBM)
SCALAR = pl.BlockSpec(memory_space=pltpu.SMEM)


def limit(mebibytes):
    return pltpu.CompilerParams(vmem_limit_bytes=mebibytes * 1024 * 1024)


def first_kernel(place_ref, in_hbm, weight_hbm, last_ref, piece_ref, weight_ref, sems):
    copies, part, lanes = piece_ref.shape
    span = last_ref.shape[1]
    y = in_hbm.shape[2] // lanes
    z_lo = weight_ref.shape[0] // part
    place = place_ref[0]
    lane = pl.multiple_of((place % y) * lanes, lanes)
    fetch_weight = pltpu.make_async_copy(
        weight_hbm.at[:, pl.ds(lane, lanes)], weight_ref, sems.at[0]
    )
    fetch_last = pltpu.make_async_copy(
        in_hbm.at[:, in_hbm.shape[1] - span :, :], last_ref, sems.at[1]
    )
    fetch_weight.start()
    fetch_last.start()
    fetch_weight.wait()
    for i in range(z_lo):

        @pl.when(place // y == i)
        def _():
            piece = weight_ref[i * part : (i + 1) * part, :].astype(jnp.bfloat16)
            for n in range(copies):
                piece_ref[n] = piece

    fetch_last.wait()


def first(inputs, weight, span):
    rows, width = weight.shape
    z_hi, z_lo, y = lax.axis_size("z_hi"), lax.axis_size("z_lo"), lax.axis_size("y")
    place = lax.axis_index(TM).astype(jnp.int32).reshape(1)
    return pl.pallas_call(
        first_kernel,
        in_specs=[SCALAR, AWAY, AWAY],
        out_specs=[NEAR, NEAR],
        out_shape=[
            jax.ShapeDtypeStruct((inputs.shape[0], span, width), inputs.dtype),
            jax.ShapeDtypeStruct((z_hi * z_lo, rows // z_lo, width // y), jnp.bfloat16),
        ],
        scratch_shapes=[
            pltpu.VMEM((rows, width // y), jnp.float32),
            pltpu.SemaphoreType.DMA((2,)),
        ],
        compiler_params=limit(4),
        name="first",
    )(place, away(inputs), away(weight))


def ready_kernel(in_hbm, early_hbm, mid_hbm, up_hbm, near_ref, mid_ref, up_ref, sems):
    span = early_hbm.shape[1]
    copies = [
        pltpu.make_async_copy(early_hbm, near_ref.at[:, :span, :], sems.at[0]),
        pltpu.make_async_copy(in_hbm, near_ref.at[:, span:, :], sems.at[1]),
        pltpu.make_async_copy(mid_hbm, mid_ref, sems.at[2]),
        pltpu.make_async_copy(up_hbm, up_ref, sems.at[3]),
    ]
    for c in copies:
        c.start()
    for c in copies:
        c.wait()


def ready(inputs, early, mid, up):
    series_n, time_n, width = inputs.shape
    long = (series_n, early.shape[1] + time_n, width)
    return pl.pallas_call(
        ready_kernel,
        in_specs=[AWAY] * 4,
        out_specs=[NEAR] * 3,
        out_shape=[
            jax.ShapeDtypeStruct(long, inputs.dtype),
            jax.ShapeDtypeStruct(mid.shape, mid.dtype),
            jax.ShapeDtypeStruct(up.shape, up.dtype),
        ],
        scratch_shapes=[pltpu.SemaphoreType.DMA((4,))],
        compiler_params=limit(4),
        name="ready",
    )(away(inputs), away(early), away(mid), away(up))


def layer_kernel(
    core_ref, mine_ref, other_ref, near_ref, mid_ref, up_ref,
    dpre_hbm, wide_hbm, keep_ref, give_ref, dpre_ref, wide_ref, acc_ref, sems,
):
    series_n, time_n, width = mid_ref.shape
    span = near_ref.shape[1] - time_n
    planes, line_rows, lanes = mine_ref.shape
    y = width // lanes
    x = planes // y
    rows = BLOCK_ROWS
    z_hi = line_rows // rows
    core = core_ref[0]

    def blocks():
        for h in range(z_hi):
            for i in range(x):
                for j in range(y):
                    yield h, (h * x + i) * 2 * rows, i * y + j, j * lanes

    own, far = core * rows, (1 - core) * rows
    for h, base, p, lane in blocks():
        here = pl.ds(pl.multiple_of(base + own, 16), rows)
        there = pl.ds(pl.multiple_of(base + far, 16), rows)
        wide_ref[here, lane : lane + lanes] = mine_ref[p, h * rows : (h + 1) * rows, :]
        wide_ref[there, lane : lane + lanes] = other_ref[p, h * rows : (h + 1) * rows, :]
    keep_wide = pltpu.make_async_copy(wide_ref, wide_hbm, sems.at[0])
    keep_wide.start()
    chunk = 128
    for s in range(series_n):
        for m in range(0, time_n, chunk):
            taken = (
                near_ref[s, span + m : span + m + chunk, :],
                mid_ref[s, m : m + chunk, :],
                near_ref[s, m : m + chunk, :],
            )
            pre = sum(
                jnp.dot(
                    t,
                    wide_ref[k * width : (k + 1) * width, :],
                    preferred_element_type=jnp.float32,
                )
                for k, t in enumerate(taken)
            )
            sig = jax.nn.sigmoid(pre)
            up = up_ref[s, m : m + chunk, :].astype(jnp.float32)
            dpre_ref[s, m : m + chunk, :] = (up * (sig * (1.0 + pre * (1.0 - sig)))).astype(
                jnp.bfloat16
            )
    keep_dpre = pltpu.make_async_copy(dpre_ref, dpre_hbm, sems.at[1])
    keep_dpre.start()
    for k in range(3):
        for s in range(series_n):
            taken = (near_ref[s, span:, :], mid_ref[s], near_ref[s, :time_n, :])[k]
            part = lax.dot_general(
                taken,
                dpre_ref[s],
                (((0,), (0,)), ((), ())),
                preferred_element_type=jnp.float32,
            )
            if s == 0:
                acc_ref[k * width : (k + 1) * width, :] = part
            else:
                acc_ref[k * width : (k + 1) * width, :] += part
    for h, base, p, lane in blocks():
        here = pl.ds(pl.multiple_of(base + own, 8), rows)
        there = pl.ds(pl.multiple_of(base + far, 8), rows)
        keep_ref[p, h * rows : (h + 1) * rows, :] = acc_ref[here, lane : lane + lanes]
        give_ref[p, h * rows : (h + 1) * rows, :] = acc_ref[there, lane : lane + lanes]
    keep_wide.wait()
    keep_dpre.wait()


def layer(core, mine, other, near, mid, up):
    planes, line_rows, lanes = mine.shape
    width = up.shape[-1]
    total = 2 * planes * line_rows * lanes // width
    half = jax.ShapeDtypeStruct(mine.shape, jnp.float32)
    return pl.pallas_call(
        layer_kernel,
        in_specs=[SCALAR] + [NEAR] * 5,
        out_specs=[AWAY, AWAY, NEAR, NEAR],
        out_shape=[
            pltpu.HBM(up.shape, jnp.bfloat16),
            pltpu.HBM((total, width), jnp.bfloat16),
            half,
            half,
        ],
        scratch_shapes=[
            pltpu.VMEM(up.shape, jnp.bfloat16),
            pltpu.VMEM((total, width), jnp.bfloat16),
            pltpu.VMEM((total, width), jnp.float32),
            pltpu.SemaphoreType.DMA((2,)),
        ],
        compiler_params=limit(16),
        name="layer",
    )(core, mine, other, near, mid, up)


def spread(first, second, third, wide_ref, up):
    width = up.shape[-1]
    result = up.astype(jnp.float32)
    for k, t in enumerate((first, second, third)):
        result = result + lax.dot_general(
            t,
            wide_ref[k * width : (k + 1) * width, :],
            (((1,), (1,)), ((), ())),
            preferred_element_type=jnp.float32,
        )
    return result.astype(jnp.bfloat16)


def main_kernel(dpre_ref, mid_ref, wide_ref, up_ref, out_hbm, out_ref, sem):
    series_n, time_n, _ = dpre_ref.shape
    rows = mid_ref.shape[1]
    for s in range(series_n):
        out_ref[s] = spread(
            dpre_ref[s, :rows, :],
            mid_ref[s],
            dpre_ref[s, time_n - rows :, :],
            wide_ref,
            up_ref[s, :rows, :],
        )
    out = pltpu.make_async_copy(out_ref, out_hbm.at[:, :rows, :], sem)
    out.start()
    out.wait()


def tail_kernel(dpre_ref, mid_ref, ahead_ref, wide_ref, up_ref, part_hbm, out_hbm, out_ref, sem):
    series_n, time_n, _ = dpre_ref.shape
    rows = mid_ref.shape[1]
    for s in range(series_n):
        out_ref[s] = spread(
            dpre_ref[s, time_n - rows :, :],
            mid_ref[s],
            ahead_ref[s],
            wide_ref,
            up_ref[s, time_n - rows :, :],
        )
    out = pltpu.make_async_copy(out_ref, out_hbm.at[:, time_n - rows :, :], sem)
    out.start()
    out.wait()


def input_grad(kernel, operands, mid, aliases, name):
    specs = [NEAR] * len(operands)
    if aliases:
        specs[-1] = AWAY
    return pl.pallas_call(
        kernel,
        in_specs=specs,
        out_specs=AWAY,
        out_shape=jax.ShapeDtypeStruct(operands[0].shape, jnp.bfloat16),
        scratch_shapes=[pltpu.VMEM(mid.shape, jnp.bfloat16), pltpu.SemaphoreType.DMA],
        input_output_aliases=aliases,
        compiler_params=limit(8),
        name=name,
    )(*operands)


def reduce_grad(keep, give, rows):
    z_hi, z_lo, y = lax.axis_size("z_hi"), lax.axis_size("z_lo"), lax.axis_size("y")
    lanes = keep.shape[-1]
    chunks = (keep + swapped(give)).astype(jnp.bfloat16)
    plane = jnp.sum(lax.all_to_all(chunks, PLANE, 0, 0).astype(jnp.float32), 0)
    line = plane.reshape(z_hi * z_lo, rows // z_lo, lanes)
    piece = jnp.sum(lax.all_to_all(line, LINE, 0, 0), 0)
    pieces = gathered(piece, TM).reshape(z_lo, y, rows // z_lo, lanes)
    return pieces.transpose(0, 2, 1, 3).reshape(rows, y * lanes), plane


def adamw(weight, grad, moment_one, second_moment_state):
    first = 0.9 * moment_one + 0.1 * grad
    second = 0.999 * second_moment_state + 0.001 * grad * grad
    unbiased_one = first / (1.0 - 0.9**10)
    unbiased_two = second / (1.0 - 0.999**10)
    updated = weight - 0.01 * (unbiased_one / (jnp.sqrt(unbiased_two) + 1e-08) + 0.1 * weight)
    return (updated, first, second)


def body(inputs, cotangent, taps, weight, moment_one, second_moment_state):
    time_n = inputs.shape[1]
    span = 2 * DILATION_GAP
    kept = time_n - span
    core = lax.axis_index("core").astype(jnp.int32).reshape(1)
    last, piece = first(inputs, weight, span)
    early = passed_along(last, 1)
    line, early = lax.optimization_barrier((lax.all_to_all(piece, LINE, 0, 0), early))
    mid = lax.dynamic_slice_in_dim(
        jnp.concatenate([early, inputs], 1), span - taps[1], time_n, 1
    )
    mine = gathered(line.reshape(-1, line.shape[-1]), PLANE)
    mine, early, mid, core = lax.optimization_barrier((mine, early, mid, core))
    other = swapped(mine)
    near, mid, up = ready(inputs, early, mid, cotangent)
    dpre, wide, keep, give = layer(core, mine, other, near, mid, up)
    grad_shard, plane = reduce_grad(keep, give, weight.shape[0])
    dpre, plane = lax.optimization_barrier((dpre, plane))
    mid = lax.dynamic_slice_in_dim(dpre, taps[1], kept, 1)
    part = input_grad(main_kernel, (dpre, mid, wide, cotangent), mid, {}, "main")
    head, part = lax.optimization_barrier((dpre[:, :span, :], part))
    ahead = passed_along(head, -1)
    mid = lax.dynamic_slice_in_dim(
        jnp.concatenate([dpre[:, kept:, :], ahead], 1), taps[1], span, 1
    )
    grad_input = input_grad(
        tail_kernel, (dpre, mid, ahead, wide, cotangent, part), mid, {5: 0}, "tail"
    )
    new_weight, new_moment_one, new_moment_two = adamw(
        weight, grad_shard, moment_one, second_moment_state
    )
    return (grad_input, new_weight, new_moment_one, new_moment_two)


def solution(mesh):
    torus = Mesh(mesh.devices.reshape(4, 4, 4, 4, 2), TM + SERIES)
    tokens = P(SERIES, TM, None)
    rows = P(SERIES, None)
    return jax.shard_map(
        body,
        mesh=torus,
        in_specs=(tokens, tokens, P(), rows, rows, rows),
        out_specs=(tokens, rows, rows, rows),
        check_vma=False,
    )
```

```python
import jax
import jax.numpy as jnp
from jax import lax
from jax.experimental import pallas as pl
from jax.experimental.pallas import tpu as pltpu
from jax.sharding import Mesh
from jax.sharding import PartitionSpec as P

DILATION_GAP = 64
TM = ("z_lo", "y")
SERIES = ("z_hi", "x", "core")
PLANE = ("x", "y")
LINE = ("z_hi", "z_lo")
BLOCK_ROWS = 48


def passed_along(array, by):
    size = lax.axis_size(TM)
    pairs = [(i, i + by) for i in range(size) if 0 <= i + by < size]
    return lax.ppermute(array, TM, pairs)


def gathered(piece, axes):
    size = lax.axis_size(axes)
    return lax.all_to_all(jnp.broadcast_to(piece[None], (size,) + piece.shape), axes, 0, 0)


def swapped(array):
    return lax.ppermute(array, "core", [(0, 1), (1, 0)])


def away(array):
    return pltpu.with_memory_space_constraint(array, pltpu.HBM)


COVER = pl.CostEstimate(flops=1 << 36, bytes_accessed=1 << 30, transcendentals=0)
NEAR = pl.BlockSpec(memory_space=pltpu.VMEM)
AWAY = pl.BlockSpec(memory_space=pltpu.HBM)
SCALAR = pl.BlockSpec(memory_space=pltpu.SMEM)


def limit(mebibytes):
    return pltpu.CompilerParams(vmem_limit_bytes=mebibytes * 1024 * 1024)


def first_kernel(place_ref, in_hbm, weight_hbm, last_ref, piece_ref, weight_ref, sems):
    copies, part, lanes = piece_ref.shape
    span = last_ref.shape[1]
    y = in_hbm.shape[2] // lanes
    z_lo = weight_ref.shape[0] // part
    place = place_ref[0]
    lane = pl.multiple_of((place % y) * lanes, lanes)
    fetch_weight = pltpu.make_async_copy(
        weight_hbm.at[:, pl.ds(lane, lanes)], weight_ref, sems.at[0]
    )
    fetch_last = pltpu.make_async_copy(
        in_hbm.at[:, in_hbm.shape[1] - span :, :], last_ref, sems.at[1]
    )
    fetch_weight.start()
    fetch_last.start()
    fetch_weight.wait()
    for i in range(z_lo):

        @pl.when(place // y == i)
        def _():
            piece = weight_ref[i * part : (i + 1) * part, :].astype(jnp.bfloat16)
            for n in range(copies):
                piece_ref[n] = piece

    fetch_last.wait()


def first(inputs, weight, span):
    rows, width = weight.shape
    z_hi, z_lo, y = lax.axis_size("z_hi"), lax.axis_size("z_lo"), lax.axis_size("y")
    place = lax.axis_index(TM).astype(jnp.int32).reshape(1)
    return pl.pallas_call(
        first_kernel,
        in_specs=[SCALAR, AWAY, AWAY],
        out_specs=[NEAR, NEAR],
        out_shape=[
            jax.ShapeDtypeStruct((inputs.shape[0], span, width), inputs.dtype),
            jax.ShapeDtypeStruct((z_hi * z_lo, rows // z_lo, width // y), jnp.bfloat16),
        ],
        scratch_shapes=[
            pltpu.VMEM((rows, width // y), jnp.float32),
            pltpu.SemaphoreType.DMA((2,)),
        ],
        compiler_params=limit(4),
        name="first",
    )(place, away(inputs), away(weight))


def spread_kernel(line_ref, out_ref, plane_ref):
    devices, part, _ = line_ref.shape
    for n in range(devices):
        plane_ref[n * part : (n + 1) * part, :] = line_ref[n]
    for n in range(out_ref.shape[0]):
        out_ref[n] = plane_ref[...]


def spread(line, copies):
    devices, part, lanes = line.shape
    return pl.pallas_call(
        spread_kernel,
        in_specs=[NEAR],
        out_specs=NEAR,
        out_shape=jax.ShapeDtypeStruct((copies, devices * part, lanes), line.dtype),
        scratch_shapes=[pltpu.VMEM((devices * part, lanes), line.dtype)],
        compiler_params=limit(4),
        name="spread",
    )(line)


def selector(shift, rows):
    at = lax.broadcasted_iota(jnp.int32, (rows, 2 * rows), 1)
    row = lax.broadcasted_iota(jnp.int32, (rows, 2 * rows), 0)
    return jnp.where(at == row + shift, 1.0, 0.0).astype(jnp.bfloat16)


def picked(choose, block):
    return jnp.dot(choose, block, preferred_element_type=jnp.float32).astype(jnp.bfloat16)


def ready_kernel(taps_ref, in_hbm, early_hbm, up_hbm, near_ref, mid_ref, up_ref, sems):
    series_n, time_n, _ = in_hbm.shape
    span = early_hbm.shape[1]
    copies = [
        pltpu.make_async_copy(early_hbm, near_ref.at[:, :span, :], sems.at[0]),
        pltpu.make_async_copy(in_hbm, near_ref.at[:, span:, :], sems.at[1]),
        pltpu.make_async_copy(up_hbm, up_ref, sems.at[2]),
    ]
    for c in copies:
        c.start()
    choose = selector(span - taps_ref[1], span)
    for c in copies[:2]:
        c.wait()
    for s in range(series_n):
        for m in range(0, time_n, span):
            mid_ref[s, m : m + span, :] = picked(choose, near_ref[s, m : m + 2 * span, :])
    copies[2].wait()


def ready(taps, inputs, early, up):
    series_n, time_n, width = inputs.shape
    long = (series_n, early.shape[1] + time_n, width)
    return pl.pallas_call(
        ready_kernel,
        in_specs=[SCALAR] + [AWAY] * 3,
        out_specs=[NEAR] * 3,
        out_shape=[
            jax.ShapeDtypeStruct(long, inputs.dtype),
            jax.ShapeDtypeStruct(inputs.shape, inputs.dtype),
            jax.ShapeDtypeStruct(up.shape, up.dtype),
        ],
        scratch_shapes=[pltpu.SemaphoreType.DMA((3,))],
        compiler_params=limit(8),
        name="ready",
    )(taps, away(inputs), away(early), away(up))


def layer_kernel(
    core_ref, mine_ref, other_ref, near_ref, mid_ref, up_ref,
    dpre_hbm, head_ref, wide_ref, keep_ref, give_ref, dpre_ref, acc_ref, sems,
):
    series_n, time_n, width = mid_ref.shape
    span = near_ref.shape[1] - time_n
    planes, line_rows, lanes = mine_ref.shape
    y = width // lanes
    x = planes // y
    rows = BLOCK_ROWS
    z_hi = line_rows // rows
    core = core_ref[0]

    def blocks():
        for h in range(z_hi):
            for i in range(x):
                for j in range(y):
                    yield h, (h * x + i) * 2 * rows, i * y + j, j * lanes

    own, far = core * rows, (1 - core) * rows
    for h, base, p, lane in blocks():
        here = pl.ds(pl.multiple_of(base + own, 16), rows)
        there = pl.ds(pl.multiple_of(base + far, 16), rows)
        wide_ref[here, lane : lane + lanes] = mine_ref[p, h * rows : (h + 1) * rows, :]
        wide_ref[there, lane : lane + lanes] = other_ref[p, h * rows : (h + 1) * rows, :]
    chunk = 128
    saves = []
    for s in range(series_n):
        for m in range(0, time_n, chunk):
            taken = (
                near_ref[s, span + m : span + m + chunk, :],
                mid_ref[s, m : m + chunk, :],
                near_ref[s, m : m + chunk, :],
            )
            pre = sum(
                jnp.dot(
                    t,
                    wide_ref[k * width : (k + 1) * width, :],
                    preferred_element_type=jnp.float32,
                )
                for k, t in enumerate(taken)
            )
            sig = jax.nn.sigmoid(pre)
            up = up_ref[s, m : m + chunk, :].astype(jnp.float32)
            dpre_ref[s, m : m + chunk, :] = (up * (sig * (1.0 + pre * (1.0 - sig)))).astype(
                jnp.bfloat16
            )
        head_ref[s] = dpre_ref[s, :span, :]
        saves.append(pltpu.make_async_copy(dpre_ref.at[s], dpre_hbm.at[s], sems.at[s]))
        saves[-1].start()
    for k in range(3):
        for s in range(series_n):
            taken = (near_ref[s, span:, :], mid_ref[s], near_ref[s, :time_n, :])[k]
            part = lax.dot_general(
                taken,
                dpre_ref[s],
                (((0,), (0,)), ((), ())),
                preferred_element_type=jnp.float32,
            )
            if s == 0:
                acc_ref[k * width : (k + 1) * width, :] = part
            else:
                acc_ref[k * width : (k + 1) * width, :] += part
    for h, base, p, lane in blocks():
        here = pl.ds(pl.multiple_of(base + own, 8), rows)
        there = pl.ds(pl.multiple_of(base + far, 8), rows)
        keep_ref[p, h * rows : (h + 1) * rows, :] = acc_ref[here, lane : lane + lanes]
        give_ref[p, h * rows : (h + 1) * rows, :] = acc_ref[there, lane : lane + lanes].astype(
            jnp.bfloat16
        )

    for c in saves:
        c.wait()

def layer(core, mine, other, near, mid, up):
    planes, line_rows, lanes = mine.shape
    width = up.shape[-1]
    total = 2 * planes * line_rows * lanes // width
    return pl.pallas_call(
        layer_kernel,
        in_specs=[SCALAR] + [NEAR] * 5,
        out_specs=[AWAY] + [NEAR] * 4,
        out_shape=[
            pltpu.HBM(up.shape, jnp.bfloat16),
            jax.ShapeDtypeStruct((up.shape[0], near.shape[1] - up.shape[1], width), jnp.bfloat16),
            jax.ShapeDtypeStruct((total, width), jnp.bfloat16),
            jax.ShapeDtypeStruct(mine.shape, jnp.float32),
            jax.ShapeDtypeStruct(mine.shape, jnp.bfloat16),
        ],
        scratch_shapes=[
            pltpu.VMEM(up.shape, jnp.bfloat16),
            pltpu.VMEM((total, width), jnp.float32),
            pltpu.SemaphoreType.DMA((up.shape[0],)),
        ],
        compiler_params=limit(16),
        name="layer",
    )(core, mine, other, near, mid, up)


def back_kernel(taps_ref, dpre_ref, ahead_ref, wide_ref, up_ref, out_hbm, out_ref, sems):
    series_n, time_n, width = dpre_ref.shape
    span = ahead_ref.shape[1]
    choose = selector(taps_ref[1], span)
    outs = []
    for s in range(series_n):
        later = jnp.concatenate([dpre_ref[s, span:, :], ahead_ref[s]], 0)
        mid = [
            picked(choose, dpre_ref[s, m : m + 2 * span, :]) for m in range(0, time_n - span, span)
        ]
        mid.append(picked(choose, later[time_n - 2 * span :, :]))
        result = up_ref[s].astype(jnp.float32)
        for k, rows in enumerate((dpre_ref[s], jnp.concatenate(mid, 0), later)):
            result = result + lax.dot_general(
                rows,
                wide_ref[k * width : (k + 1) * width, :],
                (((1,), (1,)), ((), ())),
                preferred_element_type=jnp.float32,
            )
        out_ref[s] = result.astype(jnp.bfloat16)
        outs.append(pltpu.make_async_copy(out_ref.at[s], out_hbm.at[s], sems.at[s]))
        outs[-1].start()
    for c in outs:
        c.wait()


def back(taps, dpre, ahead, wide, up):
    return pl.pallas_call(
        back_kernel,
        in_specs=[SCALAR] + [NEAR] * 4,
        out_specs=AWAY,
        out_shape=pltpu.HBM(dpre.shape, jnp.bfloat16),
        scratch_shapes=[
            pltpu.VMEM(dpre.shape, jnp.bfloat16),
            pltpu.SemaphoreType.DMA((dpre.shape[0],)),
        ],
        compiler_params=limit(8),
        cost_estimate=COVER,
        name="back",
    )(taps, dpre, ahead, wide, up)


def plane_sum(keep, given, rows):
    z_hi, z_lo = lax.axis_size("z_hi"), lax.axis_size("z_lo")
    chunks = (keep + given.astype(jnp.float32)).astype(jnp.bfloat16)
    plane = jnp.sum(lax.all_to_all(chunks, PLANE, 0, 0).astype(jnp.float32), 0)
    return plane.reshape(z_hi * z_lo, rows // z_lo, keep.shape[-1])


def rows_of(piece):
    z_lo, y = lax.axis_size("z_lo"), lax.axis_size("y")
    part, lanes = piece.shape
    pieces = gathered(piece, TM).reshape(z_lo, y, part, lanes)
    return pieces.transpose(0, 2, 1, 3).reshape(z_lo * part, y * lanes)


def adamw(weight, grad, moment_one, second_moment_state):
    first = 0.9 * moment_one + 0.1 * grad
    second = 0.999 * second_moment_state + 0.001 * grad * grad
    unbiased_one = first / (1.0 - 0.9**10)
    unbiased_two = second / (1.0 - 0.999**10)
    updated = weight - 0.01 * (unbiased_one / (jnp.sqrt(unbiased_two) + 1e-08) + 0.1 * weight)
    return (updated, first, second)


def body(inputs, cotangent, taps, weight, moment_one, second_moment_state):
    span = 2 * DILATION_GAP
    core = lax.axis_index("core").astype(jnp.int32).reshape(1)
    last, piece = first(inputs, weight, span)
    early = passed_along(last, 1)
    line, early, core = lax.optimization_barrier((lax.all_to_all(piece, LINE, 0, 0), early, core))
    copies = spread(line, lax.axis_size(PLANE))
    mine = lax.all_to_all(copies, PLANE, 0, 0)
    other = swapped(mine)
    mine, early = lax.optimization_barrier((mine, early))
    near, mid, up = ready(taps, inputs, early, cotangent)
    dpre, head, wide, keep, give = layer(core, mine, other, near, mid, up)
    given = swapped(give)
    ahead = passed_along(head, -1)
    grad_input = back(taps, dpre, ahead, wide, cotangent)
    line = plane_sum(keep, given, weight.shape[0])
    line, grad_input = lax.optimization_barrier((line, grad_input))
    piece = jnp.sum(lax.all_to_all(line, LINE, 0, 0), 0)
    grad_shard = rows_of(piece)
    new_weight, new_moment_one, new_moment_two = adamw(
        weight, grad_shard, moment_one, second_moment_state
    )
    return (grad_input, new_weight, new_moment_one, new_moment_two)


def solution(mesh):
    torus = Mesh(mesh.devices.reshape(4, 4, 4, 4, 2), TM + SERIES)
    tokens = P(SERIES, TM, None)
    rows = P(SERIES, None)
    return jax.shard_map(
        body,
        mesh=torus,
        in_specs=(tokens, tokens, P(), rows, rows, rows),
        out_specs=(tokens, rows, rows, rows),
        check_vma=False,
    )
```

```python
import jax
import jax.numpy as jnp
from jax import lax
from jax.experimental import pallas as pl
from jax.experimental.pallas import tpu as pltpu
from jax.sharding import Mesh
from jax.sharding import PartitionSpec as P

DILATION_GAP = 64
TM = ("z_lo", "y")
SERIES = ("z_hi", "x", "core")
PLANE = ("x", "y")
LINE = ("z_hi", "z_lo")
BLOCK_ROWS = 48


def passed_along(array, by):
    size = lax.axis_size(TM)
    pairs = [(i, i + by) for i in range(size) if 0 <= i + by < size]
    return lax.ppermute(array, TM, pairs)


def gathered(piece, axes):
    size = lax.axis_size(axes)
    return lax.all_to_all(jnp.broadcast_to(piece[None], (size,) + piece.shape), axes, 0, 0)


def swapped(array):
    return lax.ppermute(array, "core", [(0, 1), (1, 0)])


def away(array):
    return pltpu.with_memory_space_constraint(array, pltpu.HBM)


COVER = pl.CostEstimate(flops=1 << 36, bytes_accessed=1 << 30, transcendentals=0)
NEAR = pl.BlockSpec(memory_space=pltpu.VMEM)
AWAY = pl.BlockSpec(memory_space=pltpu.HBM)
SCALAR = pl.BlockSpec(memory_space=pltpu.SMEM)


def limit(mebibytes):
    return pltpu.CompilerParams(vmem_limit_bytes=mebibytes * 1024 * 1024)


def first_kernel(place_ref, in_hbm, weight_hbm, last_ref, piece_ref, weight_ref, sems):
    copies, part, lanes = piece_ref.shape
    span = last_ref.shape[1]
    y = in_hbm.shape[2] // lanes
    z_lo = weight_ref.shape[0] // part
    place = place_ref[0]
    lane = pl.multiple_of((place % y) * lanes, lanes)
    fetch_weight = pltpu.make_async_copy(
        weight_hbm.at[:, pl.ds(lane, lanes)], weight_ref, sems.at[0]
    )
    fetch_last = pltpu.make_async_copy(
        in_hbm.at[:, in_hbm.shape[1] - span :, :], last_ref, sems.at[1]
    )
    fetch_weight.start()
    fetch_last.start()
    fetch_weight.wait()
    for i in range(z_lo):

        @pl.when(place // y == i)
        def _():
            piece = weight_ref[i * part : (i + 1) * part, :].astype(jnp.bfloat16)
            for n in range(copies):
                piece_ref[n] = piece

    fetch_last.wait()


def first(inputs, weight, span):
    rows, width = weight.shape
    z_hi, z_lo, y = lax.axis_size("z_hi"), lax.axis_size("z_lo"), lax.axis_size("y")
    place = lax.axis_index(TM).astype(jnp.int32).reshape(1)
    return pl.pallas_call(
        first_kernel,
        in_specs=[SCALAR, AWAY, AWAY],
        out_specs=[NEAR, NEAR],
        out_shape=[
            jax.ShapeDtypeStruct((inputs.shape[0], span, width), inputs.dtype),
            jax.ShapeDtypeStruct((z_hi * z_lo, rows // z_lo, width // y), jnp.bfloat16),
        ],
        scratch_shapes=[
            pltpu.VMEM((rows, width // y), jnp.float32),
            pltpu.SemaphoreType.DMA((2,)),
        ],
        compiler_params=limit(4),
        name="first",
    )(place, away(inputs), away(weight))


def spread_kernel(line_ref, out_ref, plane_ref):
    devices, part, _ = line_ref.shape
    for n in range(devices):
        plane_ref[n * part : (n + 1) * part, :] = line_ref[n]
    for n in range(out_ref.shape[0]):
        out_ref[n] = plane_ref[...]


def spread(line, copies):
    devices, part, lanes = line.shape
    return pl.pallas_call(
        spread_kernel,
        in_specs=[NEAR],
        out_specs=NEAR,
        out_shape=jax.ShapeDtypeStruct((copies, devices * part, lanes), line.dtype),
        scratch_shapes=[pltpu.VMEM((devices * part, lanes), line.dtype)],
        compiler_params=limit(4),
        cost_estimate=COVER,
        name="spread",
    )(line)


def selector(shift, rows):
    at = lax.broadcasted_iota(jnp.int32, (rows, 2 * rows), 1)
    row = lax.broadcasted_iota(jnp.int32, (rows, 2 * rows), 0)
    return jnp.where(at == row + shift, 1.0, 0.0).astype(jnp.bfloat16)


def picked(choose, block):
    return jnp.dot(choose, block, preferred_element_type=jnp.float32).astype(jnp.bfloat16)


def middle_kernel(taps_ref, in_hbm, early_ref, mid_hbm, near_ref, mid_ref, sems):
    series_n, time_n, _ = in_hbm.shape
    span = early_ref.shape[1]
    fetch = pltpu.make_async_copy(in_hbm, near_ref.at[:, span:, :], sems.at[0])
    fetch.start()
    near_ref[:, :span, :] = early_ref[...]
    choose = selector(span - taps_ref[1], span)
    fetch.wait()
    for s in range(series_n):
        for m in range(0, time_n, span):
            mid_ref[s, m : m + span, :] = picked(choose, near_ref[s, m : m + 2 * span, :])
    out = pltpu.make_async_copy(mid_ref, mid_hbm, sems.at[1])
    out.start()
    out.wait()


def middle(taps, inputs, early):
    series_n, time_n, width = inputs.shape
    long = (series_n, early.shape[1] + time_n, width)
    return pl.pallas_call(
        middle_kernel,
        in_specs=[SCALAR, AWAY, NEAR],
        out_specs=AWAY,
        out_shape=pltpu.HBM(inputs.shape, inputs.dtype),
        scratch_shapes=[
            pltpu.VMEM(long, inputs.dtype),
            pltpu.VMEM(inputs.shape, inputs.dtype),
            pltpu.SemaphoreType.DMA((2,)),
        ],
        compiler_params=limit(8),
        cost_estimate=COVER,
        name="middle",
    )(taps, away(inputs), early)


def ready_kernel(in_hbm, early_hbm, mid_hbm, up_hbm, near_ref, mid_ref, up_ref, sems):
    span = early_hbm.shape[1]
    copies = [
        pltpu.make_async_copy(early_hbm, near_ref.at[:, :span, :], sems.at[0]),
        pltpu.make_async_copy(in_hbm, near_ref.at[:, span:, :], sems.at[1]),
        pltpu.make_async_copy(mid_hbm, mid_ref, sems.at[2]),
        pltpu.make_async_copy(up_hbm, up_ref, sems.at[3]),
    ]
    for c in copies:
        c.start()
    for c in copies:
        c.wait()


def ready(inputs, early, mid, up):
    series_n, time_n, width = inputs.shape
    long = (series_n, early.shape[1] + time_n, width)
    return pl.pallas_call(
        ready_kernel,
        in_specs=[AWAY] * 4,
        out_specs=[NEAR] * 3,
        out_shape=[
            jax.ShapeDtypeStruct(long, inputs.dtype),
            jax.ShapeDtypeStruct(inputs.shape, inputs.dtype),
            jax.ShapeDtypeStruct(up.shape, up.dtype),
        ],
        scratch_shapes=[pltpu.SemaphoreType.DMA((4,))],
        compiler_params=limit(8),
        name="ready",
    )(away(inputs), away(early), away(mid), away(up))


def layer_kernel(
    core_ref, mine_ref, other_ref, near_ref, mid_ref, up_ref,
    dpre_hbm, head_ref, wide_ref, keep_ref, give_ref, dpre_ref, acc_ref, sems,
):
    series_n, time_n, width = mid_ref.shape
    span = near_ref.shape[1] - time_n
    planes, line_rows, lanes = mine_ref.shape
    y = width // lanes
    x = planes // y
    rows = BLOCK_ROWS
    z_hi = line_rows // rows
    core = core_ref[0]

    def blocks():
        for h in range(z_hi):
            for i in range(x):
                for j in range(y):
                    yield h, (h * x + i) * 2 * rows, i * y + j, j * lanes

    own, far = core * rows, (1 - core) * rows
    for h, base, p, lane in blocks():
        here = pl.ds(pl.multiple_of(base + own, 16), rows)
        there = pl.ds(pl.multiple_of(base + far, 16), rows)
        wide_ref[here, lane : lane + lanes] = mine_ref[p, h * rows : (h + 1) * rows, :]
        wide_ref[there, lane : lane + lanes] = other_ref[p, h * rows : (h + 1) * rows, :]
    chunk = 128
    saves = []
    for s in range(series_n):
        for m in range(0, time_n, chunk):
            taken = (
                near_ref[s, span + m : span + m + chunk, :],
                mid_ref[s, m : m + chunk, :],
                near_ref[s, m : m + chunk, :],
            )
            pre = sum(
                jnp.dot(
                    t,
                    wide_ref[k * width : (k + 1) * width, :],
                    preferred_element_type=jnp.float32,
                )
                for k, t in enumerate(taken)
            )
            sig = jax.nn.sigmoid(pre)
            up = up_ref[s, m : m + chunk, :].astype(jnp.float32)
            dpre_ref[s, m : m + chunk, :] = (up * (sig * (1.0 + pre * (1.0 - sig)))).astype(
                jnp.bfloat16
            )
        head_ref[s] = dpre_ref[s, :span, :]
        saves.append(pltpu.make_async_copy(dpre_ref.at[s], dpre_hbm.at[s], sems.at[s]))
        saves[-1].start()
    for k in range(3):
        for s in range(series_n):
            taken = (near_ref[s, span:, :], mid_ref[s], near_ref[s, :time_n, :])[k]
            part = lax.dot_general(
                taken,
                dpre_ref[s],
                (((0,), (0,)), ((), ())),
                preferred_element_type=jnp.float32,
            )
            if s == 0:
                acc_ref[k * width : (k + 1) * width, :] = part
            else:
                acc_ref[k * width : (k + 1) * width, :] += part
    for h, base, p, lane in blocks():
        here = pl.ds(pl.multiple_of(base + own, 8), rows)
        there = pl.ds(pl.multiple_of(base + far, 8), rows)
        keep_ref[p, h * rows : (h + 1) * rows, :] = acc_ref[here, lane : lane + lanes]
        give_ref[p, h * rows : (h + 1) * rows, :] = acc_ref[there, lane : lane + lanes].astype(
            jnp.bfloat16
        )

    for c in saves:
        c.wait()

def layer(core, mine, other, near, mid, up):
    planes, line_rows, lanes = mine.shape
    width = up.shape[-1]
    total = 2 * planes * line_rows * lanes // width
    return pl.pallas_call(
        layer_kernel,
        in_specs=[SCALAR] + [NEAR] * 5,
        out_specs=[AWAY] + [NEAR] * 4,
        out_shape=[
            pltpu.HBM(up.shape, jnp.bfloat16),
            jax.ShapeDtypeStruct((up.shape[0], near.shape[1] - up.shape[1], width), jnp.bfloat16),
            jax.ShapeDtypeStruct((total, width), jnp.bfloat16),
            jax.ShapeDtypeStruct(mine.shape, jnp.float32),
            jax.ShapeDtypeStruct(mine.shape, jnp.bfloat16),
        ],
        scratch_shapes=[
            pltpu.VMEM(up.shape, jnp.bfloat16),
            pltpu.VMEM((total, width), jnp.float32),
            pltpu.SemaphoreType.DMA((up.shape[0],)),
        ],
        compiler_params=limit(16),
        name="layer",
    )(core, mine, other, near, mid, up)


def back_kernel(taps_ref, dpre_ref, ahead_ref, wide_ref, up_ref, out_hbm, out_ref, sems):
    series_n, time_n, width = dpre_ref.shape
    span = ahead_ref.shape[1]
    choose = selector(taps_ref[1], span)
    outs = []
    for s in range(series_n):
        later = jnp.concatenate([dpre_ref[s, span:, :], ahead_ref[s]], 0)
        mid = [
            picked(choose, dpre_ref[s, m : m + 2 * span, :]) for m in range(0, time_n - span, span)
        ]
        mid.append(picked(choose, later[time_n - 2 * span :, :]))
        result = up_ref[s].astype(jnp.float32)
        for k, rows in enumerate((dpre_ref[s], jnp.concatenate(mid, 0), later)):
            result = result + lax.dot_general(
                rows,
                wide_ref[k * width : (k + 1) * width, :],
                (((1,), (1,)), ((), ())),
                preferred_element_type=jnp.float32,
            )
        out_ref[s] = result.astype(jnp.bfloat16)
        outs.append(pltpu.make_async_copy(out_ref.at[s], out_hbm.at[s], sems.at[s]))
        outs[-1].start()
    for c in outs:
        c.wait()


def back(taps, dpre, ahead, wide, up):
    return pl.pallas_call(
        back_kernel,
        in_specs=[SCALAR] + [NEAR] * 4,
        out_specs=AWAY,
        out_shape=pltpu.HBM(dpre.shape, jnp.bfloat16),
        scratch_shapes=[
            pltpu.VMEM(dpre.shape, jnp.bfloat16),
            pltpu.SemaphoreType.DMA((dpre.shape[0],)),
        ],
        compiler_params=limit(8),
        cost_estimate=COVER,
        name="back",
    )(taps, dpre, ahead, wide, up)


def fold_kernel(chunks_ref, line_ref, sum_ref):
    devices, part, _ = line_ref.shape
    total = chunks_ref[0].astype(jnp.float32)
    for n in range(1, chunks_ref.shape[0]):
        total = total + chunks_ref[n].astype(jnp.float32)
    sum_ref[...] = total
    for n in range(devices):
        line_ref[n] = sum_ref[n * part : (n + 1) * part, :]


def fold(chunks, devices):
    _, rows, lanes = chunks.shape
    return pl.pallas_call(
        fold_kernel,
        in_specs=[NEAR],
        out_specs=NEAR,
        out_shape=jax.ShapeDtypeStruct((devices, rows // devices, lanes), jnp.float32),
        scratch_shapes=[pltpu.VMEM((rows, lanes), jnp.float32)],
        compiler_params=limit(4),
        name="fold",
    )(chunks)


def plane_sum(keep, given):
    chunks = (keep + given.astype(jnp.float32)).astype(jnp.bfloat16)
    return fold(lax.all_to_all(chunks, PLANE, 0, 0), lax.axis_size(LINE))


def rows_of(piece):
    z_lo, y = lax.axis_size("z_lo"), lax.axis_size("y")
    part, lanes = piece.shape
    pieces = gathered(piece, TM).reshape(z_lo, y, part, lanes)
    return pieces.transpose(0, 2, 1, 3).reshape(z_lo * part, y * lanes)


def adamw(weight, grad, moment_one, second_moment_state):
    first = 0.9 * moment_one + 0.1 * grad
    second = 0.999 * second_moment_state + 0.001 * grad * grad
    unbiased_one = first / (1.0 - 0.9**10)
    unbiased_two = second / (1.0 - 0.999**10)
    updated = weight - 0.01 * (unbiased_one / (jnp.sqrt(unbiased_two) + 1e-08) + 0.1 * weight)
    return (updated, first, second)


def body(inputs, cotangent, taps, weight, moment_one, second_moment_state):
    span = 2 * DILATION_GAP
    core = lax.axis_index("core").astype(jnp.int32).reshape(1)
    last, piece = first(inputs, weight, span)
    line = lax.all_to_all(piece, LINE, 0, 0)
    early = passed_along(last, 1)
    copies, core = lax.optimization_barrier((spread(line, lax.axis_size(PLANE)), core))
    mine = lax.all_to_all(copies, PLANE, 0, 0)
    mid = middle(taps, inputs, early)
    mine, early, mid = lax.optimization_barrier((mine, early, mid))
    other = swapped(mine)
    near, mid, up = ready(inputs, early, mid, cotangent)
    dpre, head, wide, keep, give = layer(core, mine, other, near, mid, up)
    given = swapped(give)
    ahead = passed_along(head, -1)
    grad_input = back(taps, dpre, ahead, wide, cotangent)
    line = plane_sum(keep, given)
    line, grad_input = lax.optimization_barrier((line, grad_input))
    piece = jnp.sum(lax.all_to_all(line, LINE, 0, 0), 0)
    grad_shard = rows_of(piece)
    new_weight, new_moment_one, new_moment_two = adamw(
        weight, grad_shard, moment_one, second_moment_state
    )
    return (grad_input, new_weight, new_moment_one, new_moment_two)


def solution(mesh):
    torus = Mesh(mesh.devices.reshape(4, 4, 4, 4, 2), TM + SERIES)
    tokens = P(SERIES, TM, None)
    rows = P(SERIES, None)
    return jax.shard_map(
        body,
        mesh=torus,
        in_specs=(tokens, tokens, P(), rows, rows, rows),
        out_specs=(tokens, rows, rows, rows),
        check_vma=False,
    )
```

```python
import jax
import jax.numpy as jnp
from jax import lax
from jax.experimental import pallas as pl
from jax.experimental.pallas import tpu as pltpu
from jax.sharding import Mesh
from jax.sharding import PartitionSpec as P

DILATION_GAP = 64
TM = ("z_lo", "y")
SERIES = ("z_hi", "x", "core")
PLANE = ("x", "y")
LINE = ("z_hi", "z_lo")
BLOCK_ROWS = 48


def passed_along(array, by):
    size = lax.axis_size(TM)
    pairs = [(i, i + by) for i in range(size) if 0 <= i + by < size]
    return lax.ppermute(array, TM, pairs)


def gathered(piece, axes):
    size = lax.axis_size(axes)
    return lax.all_to_all(jnp.broadcast_to(piece[None], (size,) + piece.shape), axes, 0, 0)


def swapped(array):
    return lax.ppermute(array, "core", [(0, 1), (1, 0)])


def away(array):
    return pltpu.with_memory_space_constraint(array, pltpu.HBM)


COVER = pl.CostEstimate(flops=1 << 36, bytes_accessed=1 << 30, transcendentals=0)
NEAR = pl.BlockSpec(memory_space=pltpu.VMEM)
AWAY = pl.BlockSpec(memory_space=pltpu.HBM)
SCALAR = pl.BlockSpec(memory_space=pltpu.SMEM)


def limit(mebibytes):
    return pltpu.CompilerParams(vmem_limit_bytes=mebibytes * 1024 * 1024)


def first_kernel(place_ref, in_hbm, weight_hbm, last_ref, piece_ref, weight_ref, sems):
    copies, part, lanes = piece_ref.shape
    span = last_ref.shape[1]
    y = in_hbm.shape[2] // lanes
    z_lo = weight_ref.shape[0] // part
    place = place_ref[0]
    lane = pl.multiple_of((place % y) * lanes, lanes)
    fetch_weight = pltpu.make_async_copy(
        weight_hbm.at[:, pl.ds(lane, lanes)], weight_ref, sems.at[0]
    )
    fetch_last = pltpu.make_async_copy(
        in_hbm.at[:, in_hbm.shape[1] - span :, :], last_ref, sems.at[1]
    )
    fetch_weight.start()
    fetch_last.start()
    fetch_weight.wait()
    for i in range(z_lo):

        @pl.when(place // y == i)
        def _():
            piece = weight_ref[i * part : (i + 1) * part, :].astype(jnp.bfloat16)
            for n in range(copies):
                piece_ref[n] = piece

    fetch_last.wait()


def first(inputs, weight, span):
    rows, width = weight.shape
    z_hi, z_lo, y = lax.axis_size("z_hi"), lax.axis_size("z_lo"), lax.axis_size("y")
    place = lax.axis_index(TM).astype(jnp.int32).reshape(1)
    return pl.pallas_call(
        first_kernel,
        in_specs=[SCALAR, AWAY, AWAY],
        out_specs=[NEAR, NEAR],
        out_shape=[
            jax.ShapeDtypeStruct((inputs.shape[0], span, width), inputs.dtype),
            jax.ShapeDtypeStruct((z_hi * z_lo, rows // z_lo, width // y), jnp.bfloat16),
        ],
        scratch_shapes=[
            pltpu.VMEM((rows, width // y), jnp.float32),
            pltpu.SemaphoreType.DMA((2,)),
        ],
        compiler_params=limit(4),
        name="first",
    )(place, away(inputs), away(weight))


def spread_kernel(line_ref, out_ref, plane_ref):
    devices, part, _ = line_ref.shape
    for n in range(devices):
        plane_ref[n * part : (n + 1) * part, :] = line_ref[n]
    for n in range(out_ref.shape[0]):
        out_ref[n] = plane_ref[...]


def spread(line, copies):
    devices, part, lanes = line.shape
    return pl.pallas_call(
        spread_kernel,
        in_specs=[NEAR],
        out_specs=NEAR,
        out_shape=jax.ShapeDtypeStruct((copies, devices * part, lanes), line.dtype),
        scratch_shapes=[pltpu.VMEM((devices * part, lanes), line.dtype)],
        compiler_params=limit(4),
        cost_estimate=COVER,
        name="spread",
    )(line)


def selector(shift, rows):
    at = lax.broadcasted_iota(jnp.int32, (rows, 2 * rows), 1)
    row = lax.broadcasted_iota(jnp.int32, (rows, 2 * rows), 0)
    return jnp.where(at == row + shift, 1.0, 0.0).astype(jnp.bfloat16)


def picked(choose, block):
    return jnp.dot(choose, block, preferred_element_type=jnp.float32).astype(jnp.bfloat16)


def middle_kernel(taps_ref, in_hbm, early_ref, mid_hbm, near_ref, mid_ref, sems):
    series_n, time_n, _ = in_hbm.shape
    span = early_ref.shape[1]
    fetch = pltpu.make_async_copy(in_hbm, near_ref.at[:, span:, :], sems.at[0])
    fetch.start()
    near_ref[:, :span, :] = early_ref[...]
    choose = selector(span - taps_ref[1], span)
    fetch.wait()
    for s in range(series_n):
        for m in range(0, time_n, span):
            mid_ref[s, m : m + span, :] = picked(choose, near_ref[s, m : m + 2 * span, :])
    out = pltpu.make_async_copy(mid_ref, mid_hbm, sems.at[1])
    out.start()
    out.wait()


def middle(taps, inputs, early):
    series_n, time_n, width = inputs.shape
    long = (series_n, early.shape[1] + time_n, width)
    return pl.pallas_call(
        middle_kernel,
        in_specs=[SCALAR, AWAY, NEAR],
        out_specs=AWAY,
        out_shape=pltpu.HBM(inputs.shape, inputs.dtype),
        scratch_shapes=[
            pltpu.VMEM(long, inputs.dtype),
            pltpu.VMEM(inputs.shape, inputs.dtype),
            pltpu.SemaphoreType.DMA((2,)),
        ],
        compiler_params=limit(8),
        cost_estimate=COVER,
        name="middle",
    )(taps, away(inputs), early)


def ready_kernel(in_hbm, early_hbm, mid_hbm, up_hbm, near_ref, mid_ref, up_ref, sems):
    span = early_hbm.shape[1]
    copies = [
        pltpu.make_async_copy(early_hbm, near_ref.at[:, :span, :], sems.at[0]),
        pltpu.make_async_copy(in_hbm, near_ref.at[:, span:, :], sems.at[1]),
        pltpu.make_async_copy(mid_hbm, mid_ref, sems.at[2]),
        pltpu.make_async_copy(up_hbm, up_ref, sems.at[3]),
    ]
    for c in copies:
        c.start()
    for c in copies:
        c.wait()


def ready(inputs, early, mid, up):
    series_n, time_n, width = inputs.shape
    long = (series_n, early.shape[1] + time_n, width)
    return pl.pallas_call(
        ready_kernel,
        in_specs=[AWAY] * 4,
        out_specs=[NEAR] * 3,
        out_shape=[
            jax.ShapeDtypeStruct(long, inputs.dtype),
            jax.ShapeDtypeStruct(inputs.shape, inputs.dtype),
            jax.ShapeDtypeStruct(up.shape, up.dtype),
        ],
        scratch_shapes=[pltpu.SemaphoreType.DMA((4,))],
        compiler_params=limit(8),
        name="ready",
    )(away(inputs), away(early), away(mid), away(up))


def layer_kernel(
    core_ref, mine_ref, other_ref, near_ref, mid_ref, up_ref,
    dpre_hbm, head_hbm, wide_ref, keep_ref, give_ref, dpre_ref, acc_ref, sems,
):
    series_n, time_n, width = mid_ref.shape
    span = near_ref.shape[1] - time_n
    planes, line_rows, lanes = mine_ref.shape
    y = width // lanes
    x = planes // y
    rows = BLOCK_ROWS
    z_hi = line_rows // rows
    core = core_ref[0]

    def blocks():
        for h in range(z_hi):
            for i in range(x):
                for j in range(y):
                    yield h, (h * x + i) * 2 * rows, i * y + j, j * lanes

    own, far = core * rows, (1 - core) * rows
    for h, base, p, lane in blocks():
        here = pl.ds(pl.multiple_of(base + own, 16), rows)
        there = pl.ds(pl.multiple_of(base + far, 16), rows)
        wide_ref[here, lane : lane + lanes] = mine_ref[p, h * rows : (h + 1) * rows, :]
        wide_ref[there, lane : lane + lanes] = other_ref[p, h * rows : (h + 1) * rows, :]
    chunk = 128
    saves = []
    for s in range(series_n):
        for m in range(0, time_n, chunk):
            taken = (
                near_ref[s, span + m : span + m + chunk, :],
                mid_ref[s, m : m + chunk, :],
                near_ref[s, m : m + chunk, :],
            )
            pre = sum(
                jnp.dot(
                    t,
                    wide_ref[k * width : (k + 1) * width, :],
                    preferred_element_type=jnp.float32,
                )
                for k, t in enumerate(taken)
            )
            sig = jax.nn.sigmoid(pre)
            up = up_ref[s, m : m + chunk, :].astype(jnp.float32)
            dpre_ref[s, m : m + chunk, :] = (up * (sig * (1.0 + pre * (1.0 - sig)))).astype(
                jnp.bfloat16
            )
        for c in (
            pltpu.make_async_copy(dpre_ref.at[s], dpre_hbm.at[s], sems.at[2 * s]),
            pltpu.make_async_copy(dpre_ref.at[s, :span, :], head_hbm.at[s], sems.at[2 * s + 1]),
        ):
            c.start()
            saves.append(c)
    for k in range(3):
        for s in range(series_n):
            taken = (near_ref[s, span:, :], mid_ref[s], near_ref[s, :time_n, :])[k]
            part = lax.dot_general(
                taken,
                dpre_ref[s],
                (((0,), (0,)), ((), ())),
                preferred_element_type=jnp.float32,
            )
            if s == 0:
                acc_ref[k * width : (k + 1) * width, :] = part
            else:
                acc_ref[k * width : (k + 1) * width, :] += part
    for h, base, p, lane in blocks():
        here = pl.ds(pl.multiple_of(base + own, 8), rows)
        there = pl.ds(pl.multiple_of(base + far, 8), rows)
        keep_ref[p, h * rows : (h + 1) * rows, :] = acc_ref[here, lane : lane + lanes]
        give_ref[p, h * rows : (h + 1) * rows, :] = acc_ref[there, lane : lane + lanes].astype(
            jnp.bfloat16
        )

    for c in saves:
        c.wait()

def layer(core, mine, other, near, mid, up):
    planes, line_rows, lanes = mine.shape
    width = up.shape[-1]
    total = 2 * planes * line_rows * lanes // width
    return pl.pallas_call(
        layer_kernel,
        in_specs=[SCALAR] + [NEAR] * 5,
        out_specs=[AWAY] * 2 + [NEAR] * 3,
        out_shape=[
            pltpu.HBM(up.shape, jnp.bfloat16),
            pltpu.HBM((up.shape[0], near.shape[1] - up.shape[1], width), jnp.bfloat16),
            jax.ShapeDtypeStruct((total, width), jnp.bfloat16),
            jax.ShapeDtypeStruct(mine.shape, jnp.float32),
            jax.ShapeDtypeStruct(mine.shape, jnp.bfloat16),
        ],
        scratch_shapes=[
            pltpu.VMEM(up.shape, jnp.bfloat16),
            pltpu.VMEM((total, width), jnp.float32),
            pltpu.SemaphoreType.DMA((2 * up.shape[0],)),
        ],
        compiler_params=limit(16),
        name="layer",
    )(core, mine, other, near, mid, up)


def back_kernel(taps_ref, dpre_ref, ahead_ref, wide_ref, up_ref, out_hbm, out_ref, sems):
    series_n, time_n, width = dpre_ref.shape
    span = ahead_ref.shape[1]
    choose = selector(taps_ref[1], span)
    outs = []
    for s in range(series_n):
        later = jnp.concatenate([dpre_ref[s, span:, :], ahead_ref[s]], 0)
        mid = [
            picked(choose, dpre_ref[s, m : m + 2 * span, :]) for m in range(0, time_n - span, span)
        ]
        mid.append(picked(choose, later[time_n - 2 * span :, :]))
        result = up_ref[s].astype(jnp.float32)
        for k, rows in enumerate((dpre_ref[s], jnp.concatenate(mid, 0), later)):
            result = result + lax.dot_general(
                rows,
                wide_ref[k * width : (k + 1) * width, :],
                (((1,), (1,)), ((), ())),
                preferred_element_type=jnp.float32,
            )
        out_ref[s] = result.astype(jnp.bfloat16)
        outs.append(pltpu.make_async_copy(out_ref.at[s], out_hbm.at[s], sems.at[s]))
        outs[-1].start()
    for c in outs:
        c.wait()


def back(taps, dpre, ahead, wide, up):
    return pl.pallas_call(
        back_kernel,
        in_specs=[SCALAR] + [NEAR] * 4,
        out_specs=AWAY,
        out_shape=pltpu.HBM(dpre.shape, jnp.bfloat16),
        scratch_shapes=[
            pltpu.VMEM(dpre.shape, jnp.bfloat16),
            pltpu.SemaphoreType.DMA((dpre.shape[0],)),
        ],
        compiler_params=limit(8),
        cost_estimate=COVER,
        name="back",
    )(taps, dpre, ahead, wide, up)


def fold_kernel(chunks_ref, line_ref, sum_ref):
    devices, part, _ = line_ref.shape
    total = chunks_ref[0].astype(jnp.float32)
    for n in range(1, chunks_ref.shape[0]):
        total = total + chunks_ref[n].astype(jnp.float32)
    sum_ref[...] = total
    for n in range(devices):
        line_ref[n] = sum_ref[n * part : (n + 1) * part, :]


def fold(chunks, devices):
    _, rows, lanes = chunks.shape
    return pl.pallas_call(
        fold_kernel,
        in_specs=[NEAR],
        out_specs=NEAR,
        out_shape=jax.ShapeDtypeStruct((devices, rows // devices, lanes), jnp.float32),
        scratch_shapes=[pltpu.VMEM((rows, lanes), jnp.float32)],
        compiler_params=limit(4),
        name="fold",
    )(chunks)


def plane_sum(keep, given):
    chunks = (keep + given.astype(jnp.float32)).astype(jnp.bfloat16)
    return fold(lax.all_to_all(chunks, PLANE, 0, 0), lax.axis_size(LINE))


def rows_of(piece):
    z_lo, y = lax.axis_size("z_lo"), lax.axis_size("y")
    part, lanes = piece.shape
    pieces = gathered(piece, TM).reshape(z_lo, y, part, lanes)
    return pieces.transpose(0, 2, 1, 3).reshape(z_lo * part, y * lanes)


def adamw(weight, grad, moment_one, second_moment_state):
    first = 0.9 * moment_one + 0.1 * grad
    second = 0.999 * second_moment_state + 0.001 * grad * grad
    unbiased_one = first / (1.0 - 0.9**10)
    unbiased_two = second / (1.0 - 0.999**10)
    updated = weight - 0.01 * (unbiased_one / (jnp.sqrt(unbiased_two) + 1e-08) + 0.1 * weight)
    return (updated, first, second)


def body(inputs, cotangent, taps, weight, moment_one, second_moment_state):
    span = 2 * DILATION_GAP
    core = lax.axis_index("core").astype(jnp.int32).reshape(1)
    last, piece = first(inputs, weight, span)
    line = lax.all_to_all(piece, LINE, 0, 0)
    early = passed_along(last, 1)
    copies, core = lax.optimization_barrier((spread(line, lax.axis_size(PLANE)), core))
    mine = lax.all_to_all(copies, PLANE, 0, 0)
    mid = middle(taps, inputs, early)
    mine, early, mid = lax.optimization_barrier((mine, early, mid))
    other = swapped(mine)
    near, mid, up = ready(inputs, early, mid, cotangent)
    dpre, head, wide, keep, give = layer(core, mine, other, near, mid, up)
    given = swapped(give)
    ahead = passed_along(head, -1)
    grad_input = back(taps, dpre, ahead, wide, cotangent)
    line = plane_sum(keep, given)
    line, grad_input = lax.optimization_barrier((line, grad_input))
    piece = jnp.sum(lax.all_to_all(line, LINE, 0, 0), 0)
    grad_shard = rows_of(piece)
    new_weight, new_moment_one, new_moment_two = adamw(
        weight, grad_shard, moment_one, second_moment_state
    )
    return (grad_input, new_weight, new_moment_one, new_moment_two)


def solution(mesh):
    torus = Mesh(mesh.devices.reshape(4, 4, 4, 4, 2), TM + SERIES)
    tokens = P(SERIES, TM, None)
    rows = P(SERIES, None)
    return jax.shard_map(
        body,
        mesh=torus,
        in_specs=(tokens, tokens, P(), rows, rows, rows),
        out_specs=(tokens, rows, rows, rows),
        check_vma=False,
    )
```

```python
import jax
import jax.numpy as jnp
from jax import lax
from jax.experimental import pallas as pl
from jax.experimental.pallas import tpu as pltpu
from jax.sharding import Mesh
from jax.sharding import PartitionSpec as P

DILATION_GAP = 64
TM = ("z_lo", "y")
SERIES = ("z_hi", "x", "core")
PLANE = ("x", "y")
LINE = ("z_hi", "z_lo")
BLOCK_ROWS = 48


def passed_along(array, by):
    size = lax.axis_size(TM)
    pairs = [(i, i + by) for i in range(size) if 0 <= i + by < size]
    return lax.ppermute(array, TM, pairs)


def gathered(piece, axes):
    size = lax.axis_size(axes)
    return lax.all_to_all(jnp.broadcast_to(piece[None], (size,) + piece.shape), axes, 0, 0)


def swapped(array):
    return lax.ppermute(array, "core", [(0, 1), (1, 0)])


def away(array):
    return pltpu.with_memory_space_constraint(array, pltpu.HBM)


COVER = pl.CostEstimate(flops=1 << 36, bytes_accessed=1 << 30, transcendentals=0)
NEAR = pl.BlockSpec(memory_space=pltpu.VMEM)
AWAY = pl.BlockSpec(memory_space=pltpu.HBM)
SCALAR = pl.BlockSpec(memory_space=pltpu.SMEM)


def limit(mebibytes):
    return pltpu.CompilerParams(vmem_limit_bytes=mebibytes * 1024 * 1024)


def first_kernel(place_ref, weight_hbm, piece_ref, weight_ref, sem):
    copies, part, lanes = piece_ref.shape
    z_lo = weight_ref.shape[0] // part
    y = weight_hbm.shape[1] // lanes
    place = place_ref[0]
    lane = pl.multiple_of((place % y) * lanes, lanes)
    fetch = pltpu.make_async_copy(weight_hbm.at[:, pl.ds(lane, lanes)], weight_ref, sem)
    fetch.start()
    fetch.wait()
    for i in range(z_lo):

        @pl.when(place // y == i)
        def _():
            piece = weight_ref[i * part : (i + 1) * part, :].astype(jnp.bfloat16)
            for n in range(copies):
                piece_ref[n] = piece


def first(weight):
    rows, width = weight.shape
    z_hi, z_lo, y = lax.axis_size("z_hi"), lax.axis_size("z_lo"), lax.axis_size("y")
    place = lax.axis_index(TM).astype(jnp.int32).reshape(1)
    return pl.pallas_call(
        first_kernel,
        in_specs=[SCALAR, AWAY],
        out_specs=NEAR,
        out_shape=jax.ShapeDtypeStruct((z_hi * z_lo, rows // z_lo, width // y), jnp.bfloat16),
        scratch_shapes=[pltpu.VMEM((rows, width // y), jnp.float32), pltpu.SemaphoreType.DMA],
        compiler_params=limit(4),
        name="first",
    )(place, away(weight))


def spread_kernel(line_ref, out_ref, plane_ref):
    devices, part, _ = line_ref.shape
    for n in range(devices):
        plane_ref[n * part : (n + 1) * part, :] = line_ref[n]
    for n in range(out_ref.shape[0]):
        out_ref[n] = plane_ref[...]


def spread(line, copies):
    devices, part, lanes = line.shape
    return pl.pallas_call(
        spread_kernel,
        in_specs=[NEAR],
        out_specs=NEAR,
        out_shape=jax.ShapeDtypeStruct((copies, devices * part, lanes), line.dtype),
        scratch_shapes=[pltpu.VMEM((devices * part, lanes), line.dtype)],
        compiler_params=limit(4),
        cost_estimate=COVER,
        name="spread",
    )(line)


def selector(shift, rows):
    at = lax.broadcasted_iota(jnp.int32, (rows, 2 * rows), 1)
    row = lax.broadcasted_iota(jnp.int32, (rows, 2 * rows), 0)
    return jnp.where(at == row + shift, 1.0, 0.0).astype(jnp.bfloat16)


def picked(choose, block):
    return jnp.dot(choose, block, preferred_element_type=jnp.float32).astype(jnp.bfloat16)


def middle_kernel(taps_ref, in_hbm, early_ref, mid_hbm, near_ref, mid_ref, sems):
    series_n, time_n, _ = in_hbm.shape
    span = early_ref.shape[1]
    fetch = pltpu.make_async_copy(in_hbm, near_ref.at[:, span:, :], sems.at[0])
    fetch.start()
    near_ref[:, :span, :] = early_ref[...]
    choose = selector(span - taps_ref[1], span)
    fetch.wait()
    for s in range(series_n):
        for m in range(0, time_n, span):
            mid_ref[s, m : m + span, :] = picked(choose, near_ref[s, m : m + 2 * span, :])
    out = pltpu.make_async_copy(mid_ref, mid_hbm, sems.at[1])
    out.start()
    out.wait()


def middle(taps, inputs, early):
    series_n, time_n, width = inputs.shape
    long = (series_n, early.shape[1] + time_n, width)
    return pl.pallas_call(
        middle_kernel,
        in_specs=[SCALAR, AWAY, NEAR],
        out_specs=AWAY,
        out_shape=pltpu.HBM(inputs.shape, inputs.dtype),
        scratch_shapes=[
            pltpu.VMEM(long, inputs.dtype),
            pltpu.VMEM(inputs.shape, inputs.dtype),
            pltpu.SemaphoreType.DMA((2,)),
        ],
        compiler_params=limit(8),
        cost_estimate=COVER,
        name="middle",
    )(taps, away(inputs), early)


def ready_kernel(in_hbm, early_hbm, mid_hbm, up_hbm, near_ref, mid_ref, up_ref, sems):
    span = early_hbm.shape[1]
    copies = [
        pltpu.make_async_copy(early_hbm, near_ref.at[:, :span, :], sems.at[0]),
        pltpu.make_async_copy(in_hbm, near_ref.at[:, span:, :], sems.at[1]),
        pltpu.make_async_copy(mid_hbm, mid_ref, sems.at[2]),
        pltpu.make_async_copy(up_hbm, up_ref, sems.at[3]),
    ]
    for c in copies:
        c.start()
    for c in copies:
        c.wait()


def ready(inputs, early, mid, up):
    series_n, time_n, width = inputs.shape
    long = (series_n, early.shape[1] + time_n, width)
    return pl.pallas_call(
        ready_kernel,
        in_specs=[AWAY] * 4,
        out_specs=[NEAR] * 3,
        out_shape=[
            jax.ShapeDtypeStruct(long, inputs.dtype),
            jax.ShapeDtypeStruct(inputs.shape, inputs.dtype),
            jax.ShapeDtypeStruct(up.shape, up.dtype),
        ],
        scratch_shapes=[pltpu.SemaphoreType.DMA((4,))],
        compiler_params=limit(8),
        name="ready",
    )(away(inputs), away(early), away(mid), away(up))


def layer_kernel(
    core_ref, mine_ref, other_ref, near_ref, mid_ref, up_ref,
    dpre_hbm, head_hbm, wide_ref, keep_ref, give_ref, dpre_ref, acc_ref, sems,
):
    series_n, time_n, width = mid_ref.shape
    span = near_ref.shape[1] - time_n
    planes, line_rows, lanes = mine_ref.shape
    y = width // lanes
    x = planes // y
    rows = BLOCK_ROWS
    z_hi = line_rows // rows
    core = core_ref[0]

    def blocks():
        for h in range(z_hi):
            for i in range(x):
                for j in range(y):
                    yield h, (h * x + i) * 2 * rows, i * y + j, j * lanes

    own, far = core * rows, (1 - core) * rows
    for h, base, p, lane in blocks():
        here = pl.ds(pl.multiple_of(base + own, 16), rows)
        there = pl.ds(pl.multiple_of(base + far, 16), rows)
        wide_ref[here, lane : lane + lanes] = mine_ref[p, h * rows : (h + 1) * rows, :]
        wide_ref[there, lane : lane + lanes] = other_ref[p, h * rows : (h + 1) * rows, :]
    chunk = 128
    saves = []
    for s in range(series_n):
        for m in range(0, time_n, chunk):
            taken = (
                near_ref[s, span + m : span + m + chunk, :],
                mid_ref[s, m : m + chunk, :],
                near_ref[s, m : m + chunk, :],
            )
            pre = sum(
                jnp.dot(
                    t,
                    wide_ref[k * width : (k + 1) * width, :],
                    preferred_element_type=jnp.float32,
                )
                for k, t in enumerate(taken)
            )
            sig = jax.nn.sigmoid(pre)
            up = up_ref[s, m : m + chunk, :].astype(jnp.float32)
            dpre_ref[s, m : m + chunk, :] = (up * (sig * (1.0 + pre * (1.0 - sig)))).astype(
                jnp.bfloat16
            )
        for c in (
            pltpu.make_async_copy(dpre_ref.at[s], dpre_hbm.at[s], sems.at[2 * s]),
            pltpu.make_async_copy(dpre_ref.at[s, :span, :], head_hbm.at[s], sems.at[2 * s + 1]),
        ):
            c.start()
            saves.append(c)
    for k in range(3):
        for s in range(series_n):
            taken = (near_ref[s, span:, :], mid_ref[s], near_ref[s, :time_n, :])[k]
            part = lax.dot_general(
                taken,
                dpre_ref[s],
                (((0,), (0,)), ((), ())),
                preferred_element_type=jnp.float32,
            )
            if s == 0:
                acc_ref[k * width : (k + 1) * width, :] = part
            else:
                acc_ref[k * width : (k + 1) * width, :] += part
    for h, base, p, lane in blocks():
        here = pl.ds(pl.multiple_of(base + own, 8), rows)
        there = pl.ds(pl.multiple_of(base + far, 8), rows)
        keep_ref[p, h * rows : (h + 1) * rows, :] = acc_ref[here, lane : lane + lanes]
        give_ref[p, h * rows : (h + 1) * rows, :] = acc_ref[there, lane : lane + lanes].astype(
            jnp.bfloat16
        )

    for c in saves:
        c.wait()

def layer(core, mine, other, near, mid, up):
    planes, line_rows, lanes = mine.shape
    width = up.shape[-1]
    total = 2 * planes * line_rows * lanes // width
    return pl.pallas_call(
        layer_kernel,
        in_specs=[SCALAR] + [NEAR] * 5,
        out_specs=[AWAY] * 2 + [NEAR] * 3,
        out_shape=[
            pltpu.HBM(up.shape, jnp.bfloat16),
            pltpu.HBM((up.shape[0], near.shape[1] - up.shape[1], width), jnp.bfloat16),
            jax.ShapeDtypeStruct((total, width), jnp.bfloat16),
            jax.ShapeDtypeStruct(mine.shape, jnp.float32),
            jax.ShapeDtypeStruct(mine.shape, jnp.bfloat16),
        ],
        scratch_shapes=[
            pltpu.VMEM(up.shape, jnp.bfloat16),
            pltpu.VMEM((total, width), jnp.float32),
            pltpu.SemaphoreType.DMA((2 * up.shape[0],)),
        ],
        compiler_params=limit(16),
        name="layer",
    )(core, mine, other, near, mid, up)


def back_kernel(taps_ref, dpre_ref, ahead_ref, wide_ref, up_ref, out_hbm, out_ref, sems):
    series_n, time_n, width = dpre_ref.shape
    span = ahead_ref.shape[1]
    choose = selector(taps_ref[1], span)
    outs = []
    for s in range(series_n):
        later = jnp.concatenate([dpre_ref[s, span:, :], ahead_ref[s]], 0)
        mid = [
            picked(choose, dpre_ref[s, m : m + 2 * span, :]) for m in range(0, time_n - span, span)
        ]
        mid.append(picked(choose, later[time_n - 2 * span :, :]))
        result = up_ref[s].astype(jnp.float32)
        for k, rows in enumerate((dpre_ref[s], jnp.concatenate(mid, 0), later)):
            result = result + lax.dot_general(
                rows,
                wide_ref[k * width : (k + 1) * width, :],
                (((1,), (1,)), ((), ())),
                preferred_element_type=jnp.float32,
            )
        out_ref[s] = result.astype(jnp.bfloat16)
        outs.append(pltpu.make_async_copy(out_ref.at[s], out_hbm.at[s], sems.at[s]))
        outs[-1].start()
    for c in outs:
        c.wait()


def back(taps, dpre, ahead, wide, up):
    return pl.pallas_call(
        back_kernel,
        in_specs=[SCALAR] + [NEAR] * 4,
        out_specs=AWAY,
        out_shape=pltpu.HBM(dpre.shape, jnp.bfloat16),
        scratch_shapes=[
            pltpu.VMEM(dpre.shape, jnp.bfloat16),
            pltpu.SemaphoreType.DMA((dpre.shape[0],)),
        ],
        compiler_params=limit(8),
        cost_estimate=COVER,
        name="back",
    )(taps, dpre, ahead, wide, up)


def fold_kernel(chunks_ref, line_ref, sum_ref):
    devices, part, _ = line_ref.shape
    total = chunks_ref[0].astype(jnp.float32)
    for n in range(1, chunks_ref.shape[0]):
        total = total + chunks_ref[n].astype(jnp.float32)
    sum_ref[...] = total
    for n in range(devices):
        line_ref[n] = sum_ref[n * part : (n + 1) * part, :]


def fold(chunks, devices):
    _, rows, lanes = chunks.shape
    return pl.pallas_call(
        fold_kernel,
        in_specs=[NEAR],
        out_specs=NEAR,
        out_shape=jax.ShapeDtypeStruct((devices, rows // devices, lanes), jnp.float32),
        scratch_shapes=[pltpu.VMEM((rows, lanes), jnp.float32)],
        compiler_params=limit(4),
        name="fold",
    )(chunks)


def plane_sum(keep, given):
    chunks = (keep + given.astype(jnp.float32)).astype(jnp.bfloat16)
    return fold(lax.all_to_all(chunks, PLANE, 0, 0), lax.axis_size(LINE))


def rows_of(piece):
    z_lo, y = lax.axis_size("z_lo"), lax.axis_size("y")
    part, lanes = piece.shape
    pieces = gathered(piece, TM).reshape(z_lo, y, part, lanes)
    return pieces.transpose(0, 2, 1, 3).reshape(z_lo * part, y * lanes)


def adamw(weight, grad, moment_one, second_moment_state):
    first = 0.9 * moment_one + 0.1 * grad
    second = 0.999 * second_moment_state + 0.001 * grad * grad
    unbiased_one = first / (1.0 - 0.9**10)
    unbiased_two = second / (1.0 - 0.999**10)
    updated = weight - 0.01 * (unbiased_one / (jnp.sqrt(unbiased_two) + 1e-08) + 0.1 * weight)
    return (updated, first, second)


def body(inputs, cotangent, taps, weight, moment_one, second_moment_state):
    span = 2 * DILATION_GAP
    core = lax.axis_index("core").astype(jnp.int32).reshape(1)
    line = lax.all_to_all(first(weight), LINE, 0, 0)
    early = passed_along(inputs[:, inputs.shape[1] - span :, :], 1)
    copies, core = lax.optimization_barrier((spread(line, lax.axis_size(PLANE)), core))
    mine = lax.all_to_all(copies, PLANE, 0, 0)
    mid = middle(taps, inputs, early)
    mine, early, mid = lax.optimization_barrier((mine, early, mid))
    other = swapped(mine)
    near, mid, up = ready(inputs, early, mid, cotangent)
    dpre, head, wide, keep, give = layer(core, mine, other, near, mid, up)
    given = swapped(give)
    ahead = passed_along(head, -1)
    grad_input = back(taps, dpre, ahead, wide, cotangent)
    line = plane_sum(keep, given)
    line, grad_input = lax.optimization_barrier((line, grad_input))
    piece = jnp.sum(lax.all_to_all(line, LINE, 0, 0), 0)
    grad_shard = rows_of(piece)
    new_weight, new_moment_one, new_moment_two = adamw(
        weight, grad_shard, moment_one, second_moment_state
    )
    return (grad_input, new_weight, new_moment_one, new_moment_two)


def solution(mesh):
    torus = Mesh(mesh.devices.reshape(4, 4, 4, 4, 2), TM + SERIES)
    tokens = P(SERIES, TM, None)
    rows = P(SERIES, None)
    return jax.shard_map(
        body,
        mesh=torus,
        in_specs=(tokens, tokens, P(), rows, rows, rows),
        out_specs=(tokens, rows, rows, rows),
        check_vma=False,
    )
```
